32 devices in a mesh: groups: 2 (over x), band: 16 (over z, y, core).
Axes of the slice: x: 2, y: 2, z: 4, core: 2. Of those that a mesh axis runs over, the one named last changes fastest.
Arguments:
- queries: bfloat16 [128, 80, 2560], P(('groups', 'band')), parts along dimension 0, may hold values from -7 to 7, as said below
- kv_frames: bfloat16 [4, 4, 64, 80, 2560], P('groups', None, 'band'), parts along dimension 0, may hold values from -7 to 7
- frame_mask: int32 [6], P('groups'), parts along dimension 0, may hold values 0 or 1
- col_shift: int32 [128], P('groups'), parts along dimension 0, may hold values from -4 to 4
- latent: bfloat16 [6, 128, 2560], P('groups', 'band'), parts along dimension 0, may hold values from -6 to 6
- conv_in: bfloat16 [432, 384], replicated, may hold values from -0.3125 to 0.3125
- bias_in: float32 [384], replicated, may hold values from -3 to 3
- norm_gain: float32 [384], replicated, may hold values from 0.1 to 1.9
- conv_mid: bfloat16 [3456, 384], replicated, may hold values from -0.109375 to 0.109375
- bias_mid: float32 [384], replicated, may hold values from -3 to 3
Outputs:
- attended: bfloat16 [128, 80, 2560], P(('groups', 'band')), parts along dimension 0
- decoded: bfloat16 [256, 160, 384], P(('groups', 'band')), parts along dimension 0
The draws below stay inside these ranges and needn't reach their ends.
There are 2 independent parts, one for each index of `groups`. The reference program is written for one: setup_inputs(seed, part) draws one part's arguments, and reference() takes and returns one part's arrays. A program takes and returns all parts, laid end to end along the dimension named above; an argument that names none is the same for every part. Nothing has to cross between parts.
Inputs may be any that keep to these rules, and one draw needn't show every extreme that they name: queries of a few patches may be large.
All inputs are finite; a program needn't handle non-finite values.
Results may differ from the reference program's by a relative error of at most 0.007.
Values may be sent and summed in bfloat16 or wider, within the bound.
A program may use at most 256 MiB of HBM per device.

```python
import math
import jax
import jax.numpy as jnp
from jax import lax

H = 20
HD = 128
COLS = 80
ROWS = 64
CACHED = 3
FRAMES = 4
RC = 8
SHIFT = 4
CL = 16
CH = 384
LROWS = 128
LC = 160


def draw_queries(key, part):
    shape_q = (ROWS, COLS, H * HD)
    base_draw = jnp.clip(jax.random.normal(key, shape_q, jnp.float32), -6.0, 6.0)
    return base_draw.astype(jnp.bfloat16)


def draw_kv_frames(key, part):
    shape_kv = (2, FRAMES, ROWS, COLS, H * HD)
    draw_key = jax.random.fold_in(key, 2213)
    base_draw = jnp.clip(jax.random.normal(draw_key, shape_kv, jnp.float32), -6.0, 6.0)
    return base_draw.astype(jnp.bfloat16)


def set_ends(values, key, smallest, high):
    longest = values.shape.index(max(values.shape))
    spots = []
    for shift in (0, 1):
        where = [jax.random.randint(jax.random.fold_in(key, axis), (), 0, length) for axis, length in enumerate(values.shape)]
        where[longest] = (where[longest] + shift) % values.shape[longest]
        spots.append(tuple(where))
    return values.at[spots[0]].set(smallest).at[spots[1]].set(high)


def block_levels(key, dims, shards, low, largest):
    def one(dim, parts):
        draws = jax.random.uniform(jax.random.fold_in(jax.random.fold_in(key, 6), dim), (parts,), jnp.float32, low / len(shards), largest / len(shards))
        return jnp.repeat(jnp.exp(draws), dims[dim] // parts).reshape((-1,) + (1,) * (len(dims) - dim - 1))

    level = one(*shards[0])
    for cut in shards[1:]:
        level = level * one(*cut)
    return level


def bell_draw(stream_key, dims, width, reach, cuts=(), held_as=jnp.bfloat16):
    values = width * jax.random.normal(stream_key, dims, jnp.float32)
    if cuts:
        values = values * block_levels(stream_key, dims, cuts, -0.22, 0.18)
    return jnp.clip(values, -reach, reach).astype(held_as)


def setup_inputs(seed: int = 0, part: int = 0) -> dict:
    splits = jax.random.split(jax.random.key(seed), 11)
    part_keys = jax.random.split(jax.random.fold_in(splits[10], part), 11)
    return {
        "queries": draw_queries(jax.random.fold_in(jax.random.fold_in(splits[10], part), 71), part),
        "kv_frames": draw_kv_frames(jax.random.fold_in(jax.random.fold_in(splits[10], part), 71), part),
        "frame_mask": set_ends((jax.random.randint(part_keys[2], (CACHED,), 0, 3) < 2).astype(jnp.int32), jax.random.fold_in(part_keys[2], 1), 0, 1),
        "col_shift": set_ends(jax.random.randint(part_keys[3], (ROWS,), 0 - SHIFT, SHIFT + 1), jax.random.fold_in(part_keys[3], 1), 0 - SHIFT, SHIFT).astype(jnp.int32),
        "latent": bell_draw(part_keys[4], (3, LROWS, LC * CL), 1.0, 6.0, ((1, 16),)),
        "conv_in": bell_draw(splits[5], (27 * CL, CH), (27 * CL) ** -0.5, 0.3125),
        "bias_in": bell_draw(splits[6], (CH,), 0.5, 3.0, (), jnp.float32),
        "norm_gain": jnp.clip(1.0 + 0.18 * jax.random.normal(splits[7], (CH,), jnp.float32), 0.1, 1.9),
        "conv_mid": bell_draw(splits[8], (9 * CH, CH), (9 * CH) ** -0.5, 0.109375),
        "bias_mid": bell_draw(splits[9], (CH,), 0.5, 3.0, (), jnp.float32),
    }


def attend(query_row, window, row_ok, col_offset, frame_ok):
    width_c = query_row.shape[0]
    span = window.shape[2]
    frames = window.shape[1]
    query_heads = query_row.reshape(width_c, H, HD).astype(jnp.float32)
    key_part = window[0].reshape(frames, span, width_c, H, HD).astype(jnp.float32)
    value_part = window[1].reshape(frames, span, width_c, H, HD).astype(jnp.float32)
    scores = jnp.einsum('chd,fnkhd->hcfnk', query_heads, key_part) * (1.0 / math.sqrt(HD))
    columns = jnp.arange(width_c, dtype=jnp.int32)
    column_ok = jnp.abs(columns[None, :] - columns[:, None] - col_offset) <= RC
    valid = column_ok[:, None, None, :] & frame_ok[None, :, None, None] & row_ok[None, None, :, None]
    scores = jnp.where(valid[None], scores, -1e+30)
    row_max = lax.optimization_barrier(jnp.max(scores, axis=(2, 3, 4)))
    weights = jnp.where(valid[None], jnp.exp(scores - row_max[:, :, None, None, None]), 0.0)
    row_sum = lax.optimization_barrier(jnp.sum(weights, axis=(2, 3, 4)))
    rounded = weights.astype(jnp.bfloat16).astype(jnp.float32)
    numerator = jnp.einsum('hcfnk,fnkhd->chd', rounded, value_part)
    return (numerator, row_max, row_sum)

def conv_first(source, out_rows, conv_in, bias_in):
    channels = conv_in.shape[0] // 27
    width_x = source.shape[2] // channels
    grid = source.reshape(3, source.shape[1], width_x, channels)
    grid = jnp.pad(grid, ((0, 0), (0, 0), (1, 1), (0, 0)))
    pieces = []
    for delta_t in range(3):
        for delta_y in range(3):
            for delta_x in range(3):
                pieces.append(grid[delta_t, delta_y:delta_y + out_rows, delta_x:delta_x + width_x, :])
    patches = jnp.concatenate(pieces, axis=-1).reshape(out_rows * width_x, 27 * channels)
    hidden = jnp.dot(patches, conv_in, preferred_element_type=jnp.float32) + bias_in.astype(jnp.float32)
    return hidden.reshape(out_rows, width_x, conv_in.shape[1])

def activate(hidden, norm_gain):
    scale = lax.rsqrt(lax.optimization_barrier(jnp.mean(hidden * hidden, axis=-1, keepdims=True)) + 1e-06)
    return jax.nn.silu(hidden * scale * norm_gain.astype(jnp.float32))

def conv_second(active, out_rows, conv_mid):
    width_x = active.shape[1]
    grid = jnp.pad(active, ((0, 0), (1, 1), (0, 0)))
    pieces = []
    for delta_y in range(3):
        for delta_x in range(3):
            pieces.append(grid[delta_y:delta_y + out_rows, delta_x:delta_x + width_x, :])
    patches = jnp.concatenate(pieces, axis=-1).reshape(out_rows * width_x, conv_mid.shape[0])
    result = jnp.dot(patches, conv_mid, preferred_element_type=jnp.float32)
    return result.reshape(out_rows, width_x, conv_mid.shape[1])

def reference(queries, kv_frames, frame_mask, col_shift, latent, conv_in, bias_in, norm_gain, conv_mid, bias_mid):
    total_rows = queries.shape[0]
    width_c = queries.shape[1]
    frame_ok = jnp.concatenate([frame_mask == 1, jnp.ones((1,), dtype=bool)])

    def one_row(row_at):
        start_row = jnp.clip(row_at - 1, 0, total_rows - 3).astype(jnp.int32)
        window = lax.dynamic_slice_in_dim(kv_frames, start_row, 3, 2)
        key_rows = start_row + jnp.arange(3, dtype=jnp.int32)
        row_ok = jnp.abs(key_rows - row_at) <= 1
        query_row = lax.dynamic_index_in_dim(queries, row_at, 0, keepdims=False)
        col_offset = lax.dynamic_index_in_dim(col_shift, row_at, 0, keepdims=False)
        numerator, row_max, row_sum = attend(query_row, window, row_ok, col_offset, frame_ok)
        result = numerator / jnp.transpose(row_sum)[:, :, None]
        return result.reshape(width_c, H * HD).astype(jnp.bfloat16)
    attended = lax.map(one_row, jnp.arange(total_rows, dtype=jnp.int32))
    lat_rows = latent.shape[1]
    padded_lat = jnp.pad(latent, ((0, 0), (1, 1), (0, 0)))
    first = conv_first(padded_lat, lat_rows, conv_in, bias_in)
    active = activate(first, norm_gain).astype(jnp.bfloat16)
    active = jnp.pad(active, ((1, 1), (0, 0), (0, 0)))
    decoded = (conv_second(active, lat_rows, conv_mid) + bias_mid.astype(jnp.float32) + first).astype(jnp.bfloat16)
    return (attended, decoded)
```

```python
import functools
import math

import jax
import jax.numpy as jnp
from jax import lax
from jax.experimental import pallas as pl
from jax.experimental.pallas import tpu as pltpu
from jax.sharding import PartitionSpec as P

HD = 128
RC = 8
NEG = -1e30
SCALE = 1.0 / math.sqrt(HD)
HEADS_PER_STEP = 2


def to_next(block, axis):
    count = lax.axis_size(axis)
    return lax.ppermute(block, axis, [(i, i + 1) for i in range(count - 1)])


def to_previous(block, axis):
    count = lax.axis_size(axis)
    return lax.ppermute(block, axis, [(i + 1, i) for i in range(count - 1)])


def window_bias(key_cols, frame_bias, offset, cols):
    width = key_cols.shape[1]
    query_cols = lax.broadcasted_iota(jnp.int32, (cols, width), 0)
    ok = jnp.abs(key_cols - query_cols - offset) <= RC
    return jnp.where(ok, frame_bias, NEG)


def partial_attention(query, keys, values, bias):
    scores = lax.dot_general(
        query, keys, (((1,), (1,)), ((), ())), preferred_element_type=jnp.float32
    )
    scores = scores + bias
    top = jnp.max(scores, axis=-1, keepdims=True)
    weights = jnp.exp((scores - top) * SCALE)
    total = jnp.sum(weights, axis=-1, keepdims=True)
    numerator = jnp.dot(weights.astype(jnp.bfloat16), values, preferred_element_type=jnp.float32)
    return numerator * (1.0 / total), top * SCALE + jnp.log(total)


def edge_kernel(
    offsets, cols_ref, fb_ref, qp_ref, qn_ref, kvf_ref, kvl_ref, op_ref, on_ref, lp_ref, ln_ref, bias_ref
):
    step = pl.program_id(0)
    frames, cols = kvf_ref.shape[1], qp_ref.shape[1]

    @pl.when(step == 0)
    def _():
        for side in range(2):
            bias_ref[side] = window_bias(cols_ref[...], fb_ref[...], offsets[side], cols)
        lp_ref[...] = jnp.zeros_like(lp_ref)
        ln_ref[...] = jnp.zeros_like(ln_ref)

    lane = lax.broadcasted_iota(jnp.int32, lp_ref.shape, 1)
    for j in range(HEADS_PER_STEP):
        part = pl.ds(j * HD, HD)
        sides = ((qp_ref, kvf_ref, op_ref, lp_ref), (qn_ref, kvl_ref, on_ref, ln_ref))
        for side, (q_ref, kv_ref, o_ref, l_ref) in enumerate(sides):
            keys = jnp.concatenate([kv_ref[0, f, 0, :, part] for f in range(frames)], axis=0)
            values = jnp.concatenate([kv_ref[1, f, 0, :, part] for f in range(frames)], axis=0)
            out, level = partial_attention(q_ref[0, :, part], keys, values, bias_ref[side])
            o_ref[0, :, part] = out.astype(jnp.bfloat16)
            l_ref[...] = jnp.where(lane == step * HEADS_PER_STEP + j, level, l_ref[...])


def main_kernel(
    offsets, cols_ref, fb_ref, q_ref, kv_ref, op_ref, on_ref, lp_ref, ln_ref, out_ref, bias_ref
):
    step = pl.program_id(0)
    frames, rows, cols = kv_ref.shape[1], q_ref.shape[0], q_ref.shape[1]

    @pl.when(step == 0)
    def _():
        for r in range(rows):
            bias_ref[r] = window_bias(cols_ref[...], fb_ref[...], offsets[r], cols)

    lane = lax.broadcasted_iota(jnp.int32, lp_ref.shape, 1)
    for j in range(HEADS_PER_STEP):
        part = pl.ds(j * HD, HD)
        for r in range(rows):
            near = range(max(r - 1, 0), min(r + 2, rows))
            keys = jnp.concatenate([kv_ref[0, f, n, :, part] for n in near for f in range(frames)], axis=0)
            values = jnp.concatenate([kv_ref[1, f, n, :, part] for n in near for f in range(frames)], axis=0)
            bias = bias_ref[r, :, : keys.shape[0]]
            out, level = partial_attention(q_ref[r, :, part], keys, values, bias)
            pieces = [(out, level)]
            for at, o_ref, l_ref, flag in ((0, op_ref, lp_ref, rows), (rows - 1, on_ref, ln_ref, rows + 1)):
                if r == at:
                    other = jnp.sum(
                        jnp.where(lane == step * HEADS_PER_STEP + j, l_ref[...], 0.0), axis=-1, keepdims=True
                    )
                    other = jnp.where(offsets[flag] == 1, other, NEG)
                    pieces.append((o_ref[0, :, part].astype(jnp.float32), other))
            if len(pieces) > 1:
                top = functools.reduce(jnp.maximum, [level for _, level in pieces])
                shares = [jnp.exp(level - top) for _, level in pieces]
                mixed = sum(share * piece for share, (piece, _) in zip(shares, pieces))
                out = mixed * (1.0 / sum(shares))
            out_ref[r, :, part] = out.astype(jnp.bfloat16)


def attention(queries, kv_frames, frame_mask, col_shift, place, count):
    rows, cols, wide = queries.shape
    frames = kv_frames.shape[1]
    heads = wide // HD
    step_lanes = HEADS_PER_STEP * HD
    grid = (heads // HEADS_PER_STEP,)
    first_row = place * rows
    frame_ok = jnp.concatenate([frame_mask == 1, jnp.ones((1,), dtype=bool)])
    near = min(rows, 3)
    frame_bias = jnp.tile(jnp.repeat(jnp.where(frame_ok, 0.0, NEG), cols), near)[None]
    key_cols = jnp.tile(jnp.arange(cols, dtype=jnp.int32), near * frames)[None]
    has_prev = (place > 0).astype(jnp.int32)
    has_next = (place < count - 1).astype(jnp.int32)
    own_offsets = lax.dynamic_slice_in_dim(col_shift, first_row, rows)
    total = col_shift.shape[0]
    side_rows = jnp.clip(jnp.stack([first_row - 1, first_row + rows]), 0, total - 1)
    side_offsets = col_shift[side_rows]

    q_prev = to_next(queries[rows - 1 :], "band")
    q_next = to_previous(queries[:1], "band")

    smem = pl.BlockSpec(memory_space=pltpu.SMEM)
    one = frames * cols

    def fixed(shape):
        return pl.BlockSpec(shape, lambda h: (0,) * len(shape))

    def lanes(shape, row=0):
        lead = (0,) * (len(shape) - 3)
        return pl.BlockSpec(shape, lambda h: lead + (row, 0, h))

    row_q = (1, cols, step_lanes)
    o_prev, o_next, l_prev, l_next = pl.pallas_call(
        edge_kernel,
        grid=grid,
        out_shape=(
            jax.ShapeDtypeStruct((1, cols, wide), jnp.bfloat16),
            jax.ShapeDtypeStruct((1, cols, wide), jnp.bfloat16),
            jax.ShapeDtypeStruct((cols, 128), jnp.float32),
            jax.ShapeDtypeStruct((cols, 128), jnp.float32),
        ),
        in_specs=[
            smem,
            fixed((1, one)),
            fixed((1, one)),
            lanes(row_q),
            lanes(row_q),
            lanes((2, frames, 1, cols, step_lanes), 0),
            lanes((2, frames, 1, cols, step_lanes), rows - 1),
        ],
        out_specs=(lanes(row_q), lanes(row_q), fixed((cols, 128)), fixed((cols, 128))),
        scratch_shapes=[pltpu.VMEM((2, cols, one), jnp.float32)],
        cost_estimate=pl.CostEstimate(
            flops=2 * 4 * cols * one * wide, bytes_accessed=4 * one * wide * 2, transcendentals=2 * heads * cols * one
        ),
        name="edge_attention",
    )(side_offsets, key_cols[:, :one], frame_bias[:, :one], q_prev, q_next, kv_frames, kv_frames)

    back_prev = to_next(o_next, "band")
    back_next = to_previous(o_prev, "band")
    level_prev = to_next(l_next, "band")
    level_next = to_previous(l_prev, "band")

    scalars = jnp.concatenate([own_offsets, jnp.stack([has_prev, has_next])])
    return pl.pallas_call(
        main_kernel,
        grid=grid,
        out_shape=jax.ShapeDtypeStruct(queries.shape, jnp.bfloat16),
        in_specs=[
            smem,
            fixed((1, near * one)),
            fixed((1, near * one)),
            lanes((rows, cols, step_lanes)),
            lanes((2, frames, rows, cols, step_lanes)),
            lanes(row_q),
            lanes(row_q),
            fixed((cols, 128)),
            fixed((cols, 128)),
        ],
        out_specs=lanes((rows, cols, step_lanes)),
        scratch_shapes=[pltpu.VMEM((rows, cols, near * one), jnp.float32)],
        cost_estimate=pl.CostEstimate(
            flops=4 * rows * cols * near * one * wide,
            bytes_accessed=2 * rows * one * wide * 2,
            transcendentals=rows * heads * cols * near * one,
        ),
        name="main_attention",
    )(scalars, key_cols, frame_bias, queries, kv_frames, back_prev, back_next, level_prev, level_next)


def decoder_kernel(
    group, flags, lat_ref, win_ref, wmid_ref, bin_ref, gain_ref, bmid_ref, out_ref, first_ref, act_ref
):
    width, ch = out_ref.shape[1], out_ref.shape[2]
    rows = out_ref.shape[0]
    x_at = lax.broadcasted_iota(jnp.int32, (width, ch), 0)

    @pl.loop(0, rows + 2)
    def _(i):
        source = lat_ref[i]
        left = jnp.dot(source, win_ref[0], preferred_element_type=jnp.float32)
        mid = jnp.dot(source, win_ref[1], preferred_element_type=jnp.float32)
        right = jnp.dot(source, win_ref[2], preferred_element_type=jnp.float32)
        left = jnp.where(x_at == 0, 0.0, pltpu.roll(left, 1, 0))
        right = jnp.where(x_at == width - 1, 0.0, pltpu.roll(right, width - 1, 0))
        first = left + mid + right + bin_ref[...]
        first_ref[i] = first
        scale = lax.rsqrt(jnp.mean(first * first, axis=-1, keepdims=True) + 1e-06)
        value = first * scale * gain_ref[...]
        active = value / (1.0 + jnp.exp(-value))
        outside = ((i == 0) & (flags[0] == 0)) | ((i == rows + 1) & (flags[1] == 0))
        active = jnp.where(outside, 0.0, active)
        at = pl.ds(pl.multiple_of(i * width, width), width)
        act_ref[at, 0:ch] = jnp.where(x_at == 0, 0.0, pltpu.roll(active, 1, 0)).astype(jnp.bfloat16)
        act_ref[at, ch : 2 * ch] = active.astype(jnp.bfloat16)
        act_ref[at, 2 * ch : 3 * ch] = jnp.where(
            x_at == width - 1, 0.0, pltpu.roll(active, width - 1, 0)
        ).astype(jnp.bfloat16)

    @pl.loop(0, rows // group)
    def _(g):
        total = jnp.zeros((group * width, ch), jnp.float32)
        for dy in range(3):
            at = pl.ds(pl.multiple_of((g * group + dy) * width, width), group * width)
            total += jnp.dot(
                act_ref[at, :], wmid_ref[dy * 3 * ch : (dy + 1) * 3 * ch, :], preferred_element_type=jnp.float32
            )
        total = total + bmid_ref[...]
        for y in range(group):
            here = g * group + y
            out_ref[here] = (total[y * width : (y + 1) * width] + first_ref[here + 1]).astype(jnp.bfloat16)


def decoder(latent, conv_in, bias_in, norm_gain, conv_mid, bias_mid, place, count):
    times, rows, packed = latent.shape
    ch = conv_in.shape[1]
    depth = conv_in.shape[0] // 27
    width = packed // depth
    low = to_next(latent[:, rows - 2 :], "band")
    high = to_previous(latent[:, :2], "band")
    grid_rows = jnp.concatenate([low, latent, high], axis=1)
    pixels = grid_rows.reshape(times, rows + 4, width, depth).transpose(1, 2, 0, 3)
    pixels = pixels.reshape(rows + 4, width, times * depth)
    stacked = jnp.concatenate([pixels[dy : dy + rows + 2] for dy in range(3)], axis=-1)
    weights = conv_in.reshape(3, 3, 3, depth, ch).transpose(2, 1, 0, 3, 4).reshape(3, 9 * depth, ch)
    flags = jnp.stack([(place > 0).astype(jnp.int32), (place < count - 1).astype(jnp.int32)])
    group = next(size for size in (4, 2, 1) if rows % size == 0)
    vmem = pl.BlockSpec(memory_space=pltpu.VMEM)
    return pl.pallas_call(
        functools.partial(decoder_kernel, group),
        out_shape=jax.ShapeDtypeStruct((rows, width, ch), jnp.bfloat16),
        in_specs=[pl.BlockSpec(memory_space=pltpu.SMEM)] + [vmem] * 6,
        out_specs=vmem,
        scratch_shapes=[
            pltpu.VMEM((rows + 2, width, ch), jnp.float32),
            pltpu.VMEM(((rows + 2) * width, 3 * ch), jnp.bfloat16),
        ],
        cost_estimate=pl.CostEstimate(
            flops=2 * rows * width * 9 * ch * ch, bytes_accessed=9 * ch * ch * 2, transcendentals=rows * width * ch
        ),
        name="decoder",
    )(flags, stacked, weights, conv_mid, bias_in[None], norm_gain[None], bias_mid[None])


def body(
    queries, kv_frames, frame_mask, col_shift, latent, conv_in, bias_in, norm_gain, conv_mid, bias_mid
):
    count = lax.axis_size("band")
    place = lax.axis_index("band")
    attended = attention(queries, kv_frames, frame_mask, col_shift, place, count)
    decoded = decoder(latent, conv_in, bias_in, norm_gain, conv_mid, bias_mid, place, count)
    return (attended, decoded)


def solution(mesh):
    placed = (
        P(("groups", "band"), None, None),
        P("groups", None, "band", None, None),
        P("groups"),
        P("groups"),
        P("groups", "band", None),
        P(),
        P(),
        P(),
        P(),
        P(),
    )
    return jax.shard_map(
        body,
        mesh=mesh,
        in_specs=placed,
        out_specs=(P(("groups", "band"), None, None), P(("groups", "band"), None, None)),
        check_vma=False,
    )
```

```python
import functools
import math

import jax
import jax.numpy as jnp
from jax import lax
from jax.experimental import pallas as pl
from jax.experimental.pallas import tpu as pltpu
from jax.sharding import PartitionSpec as P

HD = 128
RC = 8
NEG = -1e30
SCALE = 1.0 / math.sqrt(HD)
HEADS_PER_STEP = 4


def to_next(block, axis):
    count = lax.axis_size(axis)
    return lax.ppermute(block, axis, [(i, i + 1) for i in range(count - 1)])


def to_previous(block, axis):
    count = lax.axis_size(axis)
    return lax.ppermute(block, axis, [(i + 1, i) for i in range(count - 1)])


def fill_bias(store, copies, offset, mask, cols, frames):
    key = lax.broadcasted_iota(jnp.int32, (cols, cols), 1)
    query = lax.broadcasted_iota(jnp.int32, (cols, cols), 0)
    ok = jnp.abs(key - query - offset) <= RC
    for f in range(frames):
        open_value = jnp.where(mask[f] == 1, 0.0, NEG) if f < frames - 1 else 0.0
        piece = jnp.where(ok, open_value, NEG)
        for n in range(copies):
            at = (n * frames + f) * cols
            store(at, piece)


def score(query, keys):
    return lax.dot_general(
        query, keys, (((1,), (1,)), ((), ())), preferred_element_type=jnp.float32
    )


def soften(scores, bias):
    scores = scores + bias
    top = jnp.max(scores, axis=-1, keepdims=True)
    weights = jnp.exp((scores - top) * SCALE)
    total = jnp.sum(weights, axis=-1, keepdims=True)
    return weights.astype(jnp.bfloat16), total, top * SCALE + jnp.log(total)


def run_staggered(tasks):
    ahead = tasks[0][0]()
    for at, (_, biases, values, finish) in enumerate(tasks):
        scores = ahead
        if at + 1 < len(tasks):
            ahead = tasks[at + 1][0]()
        weights, total, level = soften(scores, biases())
        numerator = jnp.dot(weights, values(), preferred_element_type=jnp.float32)
        finish(numerator * (1.0 / total), level)


def stack_rows(kv_ref, which, rows, part):
    return jnp.concatenate(
        [kv_ref[which, f, n, :, part] for n in rows for f in range(kv_ref.shape[1])], axis=0
    )


def edge_kernel(
    total_rows, rows, shift_ref, mask_ref, qp_ref, qn_ref, kvf_ref, kvl_ref, op_ref, on_ref, bias_ref, level_ref
):
    step = pl.program_id(0)
    frames, cols = kvf_ref.shape[1], kvf_ref.shape[3]
    wide = op_ref.shape[1] - 3 * 128

    @pl.when(step == 0)
    def _():
        first_row = lax.axis_index("band") * rows
        sides = (jnp.maximum(first_row - 1, 0), jnp.minimum(first_row + rows, total_rows - 1))
        for side, row in enumerate(sides):

            def store(at, piece, side=side):
                bias_ref[side, :, at : at + cols] = piece

            fill_bias(store, 1, shift_ref[row], mask_ref, cols, frames)
        level_ref[...] = jnp.zeros_like(level_ref)

    lane = lax.broadcasted_iota(jnp.int32, (cols, 128), 1)
    tasks = []
    for side, (q_ref, kv_ref, o_ref) in enumerate(((qp_ref, kvf_ref, op_ref), (qn_ref, kvl_ref, on_ref))):
        for j in range(HEADS_PER_STEP):
            part = pl.ds(j * HD, HD)
            head = step * HEADS_PER_STEP + j

            def finish(out, level, side=side, head=head, o_ref=o_ref):
                o_ref[:, pl.ds(pl.multiple_of(head * HD, HD), HD)] = out.astype(jnp.bfloat16)
                level_ref[side] = jnp.where(lane == head, level, level_ref[side])

            tasks.append((
                lambda q_ref=q_ref, kv_ref=kv_ref, part=part: score(q_ref[:, part], stack_rows(kv_ref, 0, (0,), part)),
                lambda side=side: bias_ref[side],
                lambda kv_ref=kv_ref, part=part: stack_rows(kv_ref, 1, (0,), part),
                finish,
            ))
    run_staggered(tasks)

    @pl.when(step == pl.num_programs(0) - 1)
    def _():
        for side, o_ref in enumerate((op_ref, on_ref)):
            rest = level_ref[side]
            for k in range(3):
                piece = rest.astype(jnp.bfloat16)
                o_ref[:, wide + k * 128 : wide + (k + 1) * 128] = piece
                rest = rest - piece.astype(jnp.float32)


def main_kernel(shift_ref, mask_ref, q_ref, kv_ref, op_ref, on_ref, out_ref, bias_ref):
    step = pl.program_id(0)
    place = lax.axis_index("band")
    count = lax.axis_size("band")
    frames, rows, cols = kv_ref.shape[1], q_ref.shape[0], q_ref.shape[1]
    wide = op_ref.shape[1] - 3 * 128

    @pl.when(step == 0)
    def _():
        for r in range(rows):

            def store(at, piece, r=r):
                bias_ref[r, :, at : at + cols] = piece

            fill_bias(store, min(rows, 3), shift_ref[place * rows + r], mask_ref, cols, frames)

    lane = lax.broadcasted_iota(jnp.int32, (cols, 128), 1)
    tasks = []
    for j in range(HEADS_PER_STEP):
        part = pl.ds(j * HD, HD)
        head = step * HEADS_PER_STEP + j
        for r in range(rows):
            near = tuple(range(max(r - 1, 0), min(r + 2, rows)))
            span = len(near) * frames * cols

            def finish(out, level, r=r, part=part, head=head):
                pieces = [(out, level)]
                for at, o_ref, there in ((0, op_ref, place > 0), (rows - 1, on_ref, place < count - 1)):
                    if r == at:
                        other = sum(
                            o_ref[:, wide + k * 128 : wide + (k + 1) * 128].astype(jnp.float32) for k in range(3)
                        )
                        other = jnp.sum(jnp.where(lane == head, other, 0.0), axis=-1, keepdims=True)
                        other = jnp.where(there, other, NEG)
                        piece = o_ref[:, pl.ds(pl.multiple_of(head * HD, HD), HD)]
                        pieces.append((piece.astype(jnp.float32), other))
                if len(pieces) > 1:
                    top = functools.reduce(jnp.maximum, [level for _, level in pieces])
                    shares = [jnp.exp(level - top) for _, level in pieces]
                    mixed = sum(share * piece for share, (piece, _) in zip(shares, pieces))
                    out = mixed * (1.0 / sum(shares))
                out_ref[r, :, part] = out.astype(jnp.bfloat16)

            tasks.append((
                lambda r=r, near=near, part=part: score(q_ref[r, :, part], stack_rows(kv_ref, 0, near, part)),
                lambda r=r, span=span: bias_ref[r, :, :span],
                lambda near=near, part=part: stack_rows(kv_ref, 1, near, part),
                finish,
            ))
    run_staggered(tasks)


def attention(queries, kv_frames, frame_mask, col_shift, q_prev, q_next):
    rows, cols, wide = queries.shape
    frames = kv_frames.shape[1]
    heads = wide // HD
    step_lanes = HEADS_PER_STEP * HD
    grid = (heads // HEADS_PER_STEP,)
    near = min(rows, 3)
    smem = pl.BlockSpec(memory_space=pltpu.SMEM)
    one = frames * cols
    packed = wide + 3 * 128

    def fixed(shape):
        return pl.BlockSpec(shape, lambda h: (0,) * len(shape))

    def lanes(shape, row=0):
        lead = (0,) * (len(shape) - 3)
        return pl.BlockSpec(shape, lambda h: lead + (row, 0, h))

    row_q = pl.BlockSpec((cols, step_lanes), lambda h: (0, h))
    o_prev, o_next = pl.pallas_call(
        functools.partial(edge_kernel, col_shift.shape[0], rows),
        grid=grid,
        out_shape=(jax.ShapeDtypeStruct((cols, packed), jnp.bfloat16),) * 2,
        in_specs=[
            smem,
            smem,
            row_q,
            row_q,
            lanes((2, frames, 1, cols, step_lanes), 0),
            lanes((2, frames, 1, cols, step_lanes), rows - 1),
        ],
        out_specs=(fixed((cols, packed)),) * 2,
        scratch_shapes=[pltpu.VMEM((2, cols, one), jnp.float32), pltpu.VMEM((2, cols, 128), jnp.float32)],
        cost_estimate=pl.CostEstimate(
            flops=2 * 4 * cols * one * wide, bytes_accessed=4 * one * wide * 2, transcendentals=2 * heads * cols * one
        ),
        name="edge_attention",
    )(col_shift, frame_mask, q_prev, q_next, kv_frames, kv_frames)

    back_prev = to_next(o_next, "band")
    back_next = to_previous(o_prev, "band")

    return pl.pallas_call(
        main_kernel,
        grid=grid,
        out_shape=jax.ShapeDtypeStruct(queries.shape, jnp.bfloat16),
        in_specs=[
            smem,
            smem,
            lanes((rows, cols, step_lanes)),
            lanes((2, frames, rows, cols, step_lanes)),
            fixed((cols, packed)),
            fixed((cols, packed)),
        ],
        out_specs=lanes((rows, cols, step_lanes)),
        scratch_shapes=[pltpu.VMEM((rows, cols, near * one), jnp.float32)],
        cost_estimate=pl.CostEstimate(
            flops=4 * rows * cols * near * one * wide,
            bytes_accessed=2 * rows * one * wide * 2,
            transcendentals=rows * heads * cols * near * one,
        ),
        name="main_attention",
    )(col_shift, frame_mask, queries, kv_frames, back_prev, back_next)


def decoder_kernel(
    group, lat_ref, cin_ref, wmid_ref, bin_ref, gain_ref, bmid_ref, out_ref, win_ref, first_ref, act_ref
):
    place = lax.axis_index("band")
    count = lax.axis_size("band")
    depth = cin_ref.shape[0] // 27
    for dx in range(3):
        for dy in range(3):
            for dt in range(3):
                source_at = ((dt * 3 + dy) * 3 + dx) * depth
                at = (dy * 3 + dt) * depth
                win_ref[dx, at : at + depth] = cin_ref[source_at : source_at + depth]
    width, ch = out_ref.shape[1], out_ref.shape[2]
    rows = out_ref.shape[0]
    x_at = lax.broadcasted_iota(jnp.int32, (width, ch), 0)

    @pl.loop(0, rows + 2)
    def _(i):
        source = lat_ref[i]
        left = jnp.dot(source, win_ref[0], preferred_element_type=jnp.float32)
        mid = jnp.dot(source, win_ref[1], preferred_element_type=jnp.float32)
        right = jnp.dot(source, win_ref[2], preferred_element_type=jnp.float32)
        left = jnp.where(x_at == 0, 0.0, pltpu.roll(left, 1, 0))
        right = jnp.where(x_at == width - 1, 0.0, pltpu.roll(right, width - 1, 0))
        first = left + mid + right + bin_ref[...][None]
        first_ref[i] = first
        scale = lax.rsqrt(jnp.mean(first * first, axis=-1, keepdims=True) + 1e-06)
        value = first * scale * gain_ref[...][None]
        active = value / (1.0 + jnp.exp(-value))
        outside = ((i == 0) & (place == 0)) | ((i == rows + 1) & (place == count - 1))
        active = jnp.where(outside, 0.0, active)
        at = pl.ds(pl.multiple_of(i * width, width), width)
        act_ref[at, 0:ch] = jnp.where(x_at == 0, 0.0, pltpu.roll(active, 1, 0)).astype(jnp.bfloat16)
        act_ref[at, ch : 2 * ch] = active.astype(jnp.bfloat16)
        act_ref[at, 2 * ch : 3 * ch] = jnp.where(
            x_at == width - 1, 0.0, pltpu.roll(active, width - 1, 0)
        ).astype(jnp.bfloat16)

    @pl.loop(0, rows // group)
    def _(g):
        total = jnp.zeros((group * width, ch), jnp.float32)
        for dy in range(3):
            at = pl.ds(pl.multiple_of((g * group + dy) * width, width), group * width)
            total += jnp.dot(
                act_ref[at, :], wmid_ref[dy * 3 * ch : (dy + 1) * 3 * ch, :], preferred_element_type=jnp.float32
            )
        total = total + bmid_ref[...][None]
        for y in range(group):
            here = g * group + y
            out_ref[here] = (total[y * width : (y + 1) * width] + first_ref[here + 1]).astype(jnp.bfloat16)


def decoder(latent, conv_in, bias_in, norm_gain, conv_mid, bias_mid, low, high):
    times, rows, packed = latent.shape
    ch = conv_in.shape[1]
    depth = conv_in.shape[0] // 27
    width = packed // depth
    grid_rows = jnp.concatenate([low, latent, high], axis=1)
    pixels = grid_rows.reshape(times, rows + 4, width, depth).transpose(1, 2, 0, 3)
    pixels = pixels.reshape(rows + 4, width, times * depth)
    stacked = jnp.concatenate([pixels[dy : dy + rows + 2] for dy in range(3)], axis=-1)
    group = next(size for size in (4, 2, 1) if rows % size == 0)
    vmem = pl.BlockSpec(memory_space=pltpu.VMEM)
    return pl.pallas_call(
        functools.partial(decoder_kernel, group),
        out_shape=jax.ShapeDtypeStruct((rows, width, ch), jnp.bfloat16),
        in_specs=[vmem] * 6,
        out_specs=vmem,
        scratch_shapes=[
            pltpu.VMEM((3, 9 * depth, ch), jnp.bfloat16),
            pltpu.VMEM((rows + 2, width, ch), jnp.float32),
            pltpu.VMEM(((rows + 2) * width, 3 * ch), jnp.bfloat16),
        ],
        cost_estimate=pl.CostEstimate(
            flops=2 * rows * width * 9 * ch * ch, bytes_accessed=9 * ch * ch * 2, transcendentals=rows * width * ch
        ),
        name="decoder",
    )(stacked, conv_in, conv_mid, bias_in, norm_gain, bias_mid)


def body(
    queries, kv_frames, frame_mask, col_shift, latent, conv_in, bias_in, norm_gain, conv_mid, bias_mid
):
    rows, cols, wide = queries.shape
    times, lat_rows, lat_wide = latent.shape
    low_rows = latent[:, lat_rows - 2 :].reshape(times * 2, lat_wide)
    high_rows = latent[:, :2].reshape(times * 2, lat_wide)
    low = to_next(jnp.concatenate([queries[rows - 1], low_rows]), "band")
    high = to_previous(jnp.concatenate([queries[0], high_rows]), "band")
    attended = attention(queries, kv_frames, frame_mask, col_shift, low, high)
    low_rows = low[cols:].reshape(times, 2, lat_wide)
    high_rows = high[cols:].reshape(times, 2, lat_wide)
    decoded = decoder(latent, conv_in, bias_in, norm_gain, conv_mid, bias_mid, low_rows, high_rows)
    return (attended, decoded)


def solution(mesh):
    placed = (
        P(("groups", "band"), None, None),
        P("groups", None, "band", None, None),
        P("groups"),
        P("groups"),
        P("groups", "band", None),
        P(),
        P(),
        P(),
        P(),
        P(),
    )
    return jax.shard_map(
        body,
        mesh=mesh,
        in_specs=placed,
        out_specs=(P(("groups", "band"), None, None), P(("groups", "band"), None, None)),
        check_vma=False,
    )
```
